32 devices in a mesh: row: 4 (over z), col: 8 (over y, x, core).
Axes of the slice: x: 2, y: 2, z: 4, core: 2. Of those that a mesh axis runs over, the one named last changes fastest.
Arguments:
- features: bfloat16 [12, 4, 256, 256], P(None, 'row', 'col'), may hold values from -6 to 6
Outputs:
- schur: float32 [12, 4, 256, 6, 8, 256], P(None, 'row', None, None, 'col')
- panels: float32 [12, 4, 256, 512], P(None, 'row')
The draws below stay inside these ranges and needn't reach their ends.
All inputs are finite; a program needn't handle non-finite values.
Results may differ from the reference program's by a relative error of at most 0.0033.
Values may be sent and summed in bfloat16 or wider, within the bound.
A program may use at most 128 MiB of HBM per device.

```python
import jax
import jax.numpy as jnp
from jax import lax

TILE = 256
FEAT = 256
TR_DEV = 12
ORDER = 12288
TC_DEV = 6
N_ROW = 4
N_COL = 8


def block_levels(own_key, shape, cuts, least, largest):
    gain = 1.0
    for axis_at, parts in cuts:
        steps = jax.random.uniform(jax.random.fold_in(jax.random.fold_in(own_key, 6), axis_at), (parts,), jnp.float32, least / len(cuts), largest / len(cuts))
        gain = gain * jnp.repeat(jnp.exp(steps), shape[axis_at] // parts).reshape((-1,) + (1,) * (len(shape) - 1 - axis_at))
    return gain


def centred(rng, dims, deviation, reach, cuts=(), kind=jnp.bfloat16):
    level = block_levels(rng, dims, cuts, -0.22, 0.18) if cuts else 1.0
    entries = jax.random.normal(rng, dims, jnp.float32) * deviation * level
    return jnp.minimum(jnp.maximum(entries, -reach), reach).astype(kind)


def setup_inputs(seed: int = 0) -> dict:
    seeds = jax.random.split(jax.random.key(seed), 2)
    features = centred(seeds[0], (TR_DEV, N_ROW, TILE, FEAT), 1.0, 6.0, ((1, 4), (2, 8)))
    return dict(features=features)


kernel_gain = 2.0
epsilon = 1e-06

def kernel_block(row_feats, col_feats, row_start, col_start):
    products = jnp.dot(row_feats.astype(jnp.float32), col_feats.T.astype(jnp.float32), preferred_element_type=jnp.float32)
    values = jnp.exp(kernel_gain * (products - 1.0))
    row_index = row_start + jnp.arange(row_feats.shape[0], dtype=jnp.int32)[:, None]
    col_index = col_start + jnp.arange(col_feats.shape[0], dtype=jnp.int32)[None, :]
    return values + (row_index == col_index).astype(values.dtype)

def panel_factor(column, panel_index):
    start = panel_index * TILE
    factor = jnp.linalg.cholesky(column[start:start + TILE])
    solved = lax.linalg.triangular_solve(factor, column, left_side=False, lower=True, transpose_a=True)
    pieces = solved.reshape(ORDER // TILE, TILE, TILE)
    marker = jnp.arange(ORDER // TILE, dtype=jnp.int32)[:, None, None]
    pieces = jnp.where(marker == panel_index, factor[None], jnp.where(marker < panel_index, jnp.zeros_like(pieces), pieces))
    return pieces.reshape(ORDER, TILE)

def reference(features):
    floated = features.reshape(ORDER, FEAT).astype(jnp.float32)
    unit_rows = (floated * lax.rsqrt(lax.optimization_barrier(jnp.sum(floated * floated, axis=-1, keepdims=True)) + epsilon)).astype(jnp.bfloat16)
    front = kernel_block(unit_rows, unit_rows[:2 * TILE], jnp.int32(0), jnp.int32(0))
    first = panel_factor(front[:, :TILE], 0)
    col_next = front[:, TILE:] - jnp.dot(first, first[TILE:2 * TILE].T, precision=lax.Precision.HIGHEST)
    second = panel_factor(col_next, 1)
    both = jnp.concatenate([first, second], axis=1)

    def one_block(block_index):
        start = (block_index * TILE).astype(jnp.int32)
        row_feats = lax.dynamic_slice_in_dim(unit_rows, start, TILE, 0)
        block_kernel = kernel_block(row_feats, unit_rows, start, jnp.int32(0))
        block_panel = lax.dynamic_slice_in_dim(both, start, TILE, 0)
        return block_kernel - jnp.dot(block_panel, both.T, precision=lax.Precision.HIGHEST)
    schur = lax.map(one_block, jnp.arange(ORDER // TILE, dtype=jnp.int32)).reshape(ORDER, ORDER)
    return (schur.reshape(TR_DEV, N_ROW, TILE, TC_DEV, N_COL, TILE), both.reshape(TR_DEV, N_ROW, TILE, 2 * TILE))
```

```python
import functools
import math

import jax
import jax.numpy as jnp
from jax import lax
from jax.experimental import pallas as pl
from jax.experimental.pallas import tpu as pltpu
from jax.sharding import PartitionSpec as P

kernel_gain = 2.0
epsilon = 1e-06
LEAF = 128
SUB = 8
gain2 = kernel_gain / math.log(2.0)
BF = jnp.bfloat16
F32 = jnp.float32
NT = (((1,), (1,)), ((), ()))
NN = (((1,), (0,)), ((), ()))
TN = (((0,), (0,)), ((), ()))


def split(x):
    hi = x.astype(BF)
    return hi, (x - hi.astype(F32)).astype(BF)


def dot(a, b, dims):
    return lax.dot_general(a, b, dims, preferred_element_type=F32)


def dot3(a, b, dims):
    ah, al = a
    bh, bl = b
    return dot(ah, bh, dims) + (dot(ah, bl, dims) + dot(al, bh, dims))


def gram(a, b):
    return jnp.exp2(gain2 * dot(a, b, NT) - gain2)


def eye(n):
    return (
        lax.broadcasted_iota(jnp.int32, (n, n), 0) == lax.broadcasted_iota(jnp.int32, (n, n), 1)
    ).astype(F32)


def leaf(block):
    groups = LEAF // SUB
    ident = eye(LEAF)
    a = [block[g * SUB:(g + 1) * SUB] for g in range(groups)]
    m = [ident[g * SUB:(g + 1) * SUB] for g in range(groups)]
    sub = lax.broadcasted_iota(jnp.int32, (SUB, LEAF), 0)

    def lane(x, at):
        return jnp.broadcast_to(x[:, at:at + 1], (SUB, LEAF))

    def row(x, at):
        return jnp.broadcast_to(x[at:at + 1, :], (SUB, LEAF))

    for p in range(groups):
        ra, rm = a[p], m[p]
        c = [lane(ra, p * SUB + k) for k in range(SUB)]
        scale, ua, um, uc = [], [], [], []
        for j in range(SUB):
            r = lax.rsqrt(row(c[j], j))
            below = jnp.where(sub > j, c[j] * r, 0.0)
            wa, wm = row(ra, j) * r, row(rm, j) * r
            wc = [row(c[k], j) * r for k in range(j + 1, SUB)]
            scale.append(r)
            ua.append(wa)
            um.append(wm)
            uc.append(wc)
            for k in range(j + 1, SUB):
                c[k] = c[k] - below * wc[k - j - 1]
            ra = jnp.where(sub == j, wa, ra - below * wa)
            rm = jnp.where(sub == j, wm, rm - below * wm)
        a[p], m[p] = ra, rm
        for g in range(p + 1, groups):
            c = [lane(a[g], p * SUB + k) for k in range(SUB)]
            for j in range(SUB):
                l = c[j] * scale[j]
                for k in range(j + 1, SUB):
                    c[k] = c[k] - l * uc[j][k - j - 1]
                a[g] = a[g] - l * ua[j]
                m[g] = m[g] - l * um[j]
    return jnp.concatenate(m, axis=0)


def factor_body(front_ref, hi_ref, lo_ref, work):
    n = front_ref.shape[0]
    blocks = n // LEAF
    f = front_ref[...]
    work[:, 0:n] = gram(f, f) + eye(n)
    work[:, n:2 * n] = eye(n)

    def step(b, carry):
        here = pl.ds(pl.multiple_of(b * LEAF, LEAF), LEAF)
        inverse = leaf(work[here, here])
        for at in range(blocks):
            lo_at, up = at * LEAF, (at + 1) * LEAF

            @pl.when(b == at)
            def _():
                inv = split(inverse)
                if at:
                    work[lo_at:up, n:n + lo_at] = dot3(
                        inv, split(work[lo_at:up, n:n + lo_at]), NN
                    )
                work[lo_at:up, n + lo_at:n + up] = inverse
                if up < n:
                    right = dot3(inv, split(work[lo_at:up, up:n]), NN)
                    rs = split(right)
                    work[up:n, up:n] = work[up:n, up:n] - dot3(rs, rs, TN)
                    ms = split(work[lo_at:up, n:n + up])
                    work[up:n, n:n + up] = work[up:n, n:n + up] - dot3(rs, ms, TN)

        return carry

    lax.fori_loop(0, blocks, step, 0)
    hi, lo = split(work[:, n:2 * n])
    hi_ref[...] = hi
    lo_ref[...] = lo


def factor(front):
    n = front.shape[0]
    shape = jax.ShapeDtypeStruct((n, n), BF)
    return pl.pallas_call(
        factor_body,
        out_shape=(shape, shape),
        in_specs=[pl.BlockSpec(memory_space=pltpu.VMEM)],
        out_specs=(pl.BlockSpec(memory_space=pltpu.VMEM),) * 2,
        scratch_shapes=[pltpu.VMEM((n, 2 * n), F32)],
        cost_estimate=pl.CostEstimate(flops=int(2e10), bytes_accessed=int(5e7), transcendentals=0),
        name="factor",
    )(front)


def panel_of(points, tile_id, front, hi_ref, lo_ref, tile_len):
    n = front.shape[0]
    values = gram(points, front)
    at = lax.broadcasted_iota(jnp.int32, values.shape, 0) + tile_id * tile_len
    values = values + (at == lax.broadcasted_iota(jnp.int32, values.shape, 1)).astype(F32)
    hi, lo = split(values)
    t = tile_len
    first = dot3((hi[:, :t], lo[:, :t]), (hi_ref[:t, :t], lo_ref[:t, :t]), NT)
    second = dot3((hi, lo), (hi_ref[t:, :], lo_ref[t:, :]), NT)
    return jnp.concatenate([first, second], axis=1)


def schur_body(ids, rows_ref, cols_ref, front_ref, hi_ref, lo_ref, out_ref, panel_ref, q_ref):
    tile_len = rows_ref.shape[0]
    across = cols_ref.shape[0] // tile_len
    own_row, row_count, own_col, col_count = ids[0], ids[1], ids[2], ids[3]
    a = pl.program_id(0)
    chunks = across * tile_len // LEAF

    @pl.when(a == 0)
    def _():
        def one(b, carry):
            here = pl.ds(pl.multiple_of(b * tile_len, tile_len), tile_len)
            hi, lo = split(
                panel_of(
                    cols_ref[here, :], b * col_count + own_col, front_ref[...], hi_ref, lo_ref,
                    tile_len,
                )
            )
            q_ref[here, :] = jnp.concatenate([hi, lo[:, :LEAF], hi[:, :LEAF]], axis=1)
            return carry

        lax.fori_loop(0, across, one, 0)

    tile_id = a * row_count + own_row
    points = rows_ref[...]
    panel = panel_of(points, tile_id, front_ref[...], hi_ref, lo_ref, tile_len)
    panel_ref[...] = panel
    hi, lo = split(panel)
    p = jnp.concatenate([hi, hi[:, :LEAF], lo[:, :LEAF]], axis=1)
    per = tile_len // LEAF
    for b in range(across):
        here = slice(b * tile_len, (b + 1) * tile_len)
        s = gram(points, cols_ref[here, :]) - dot(p, q_ref[here, :], NT)
        for k in range(per):
            out_ref[pl.ds(b * per + k, tile_len, stride=chunks), :] = s[:, k * LEAF:(k + 1) * LEAF]

        @pl.when(tile_id == b * col_count + own_col)
        def _():
            ident = eye(tile_len)
            for k in range(per):
                at = pl.ds(b * per + k, tile_len, stride=chunks)
                out_ref[at, :] = out_ref[at, :] + ident[:, k * LEAF:(k + 1) * LEAF]


def schur(ids, row_points, col_points, front, hi, lo, tile_len):
    rows, feat = row_points.shape
    cols = col_points.shape[0]
    n = front.shape[0]
    chunks = cols // LEAF

    def whole(shape):
        return pl.BlockSpec(shape, lambda a, ids: (0, 0))

    return pl.pallas_call(
        schur_body,
        out_shape=(
            jax.ShapeDtypeStruct((rows * chunks, LEAF), F32),
            jax.ShapeDtypeStruct((rows, n), F32),
        ),
        grid_spec=pltpu.PrefetchScalarGridSpec(
            num_scalar_prefetch=1,
            grid=(rows // tile_len,),
            in_specs=[
                pl.BlockSpec((tile_len, feat), lambda a, ids: (a, 0)),
                whole((cols, feat)),
                whole((n, feat)),
                whole((n, n)),
                whole((n, n)),
            ],
            out_specs=(
                pl.BlockSpec((tile_len * chunks, LEAF), lambda a, ids: (a, 0)),
                pl.BlockSpec((tile_len, n), lambda a, ids: (a, 0)),
            ),
            scratch_shapes=[pltpu.VMEM((cols, n + 2 * LEAF), BF)],
        ),
        compiler_params=pltpu.CompilerParams(dimension_semantics=("arbitrary",)),
        name="schur",
    )(ids, row_points, col_points, front, hi, lo)


def per_device(features):
    row_count = lax.axis_size("row")
    col_count = lax.axis_size("col")
    own_row = lax.axis_index("row")
    own_col = lax.axis_index("col")
    floated = features.astype(F32)
    unit = (
        floated * lax.rsqrt(jnp.sum(floated * floated, axis=-1, keepdims=True) + epsilon)
    ).astype(BF)
    leading = lax.all_gather(unit[0, 0], ("row", "col"))
    piece, feat = leading.shape[1:]
    local_tiles = unit.shape[0]
    tile_len = piece * col_count
    front = leading.reshape(row_count * tile_len, feat)[:2 * tile_len]
    hi, lo = factor(front)
    gathered = lax.all_gather(unit, "col", axis=2, tiled=True)
    stride = col_count // row_count
    grouped = gathered.reshape(local_tiles // stride, stride, tile_len, feat)
    chosen = lax.dynamic_index_in_dim(grouped, own_col // row_count, 1, keepdims=False)
    kept = jnp.where(own_row == own_col % row_count, chosen, 0).astype(BF)
    col_points = lax.psum(kept, "row").reshape(-1, feat)
    row_points = gathered.reshape(-1, feat)
    ids = jnp.stack(
        [own_row, jnp.int32(row_count), own_col, jnp.int32(col_count)]
    ).astype(jnp.int32)
    big, panels = schur(ids, row_points, col_points, front, hi, lo, tile_len)
    across = col_points.shape[0] // tile_len
    return (
        big.reshape(local_tiles, 1, tile_len, across, 1, tile_len),
        panels.reshape(local_tiles, 1, tile_len, 2 * tile_len),
    )


def solution(mesh):
    return jax.shard_map(
        per_device,
        mesh=mesh,
        in_specs=(P(None, "row", "col", None),),
        out_specs=(P(None, "row", None, None, "col", None), P(None, "row", None, None)),
        check_vma=False,
    )
```

```python
import math

import jax
import jax.numpy as jnp
from jax import lax
from jax.experimental import pallas as pl
from jax.experimental.pallas import tpu as pltpu
from jax.sharding import PartitionSpec as P

kernel_gain = 2.0
epsilon = 1e-06
LEAF = 128
SUB = 8
gain2 = kernel_gain / math.log(2.0)
BF = jnp.bfloat16
F32 = jnp.float32
NT = (((1,), (1,)), ((), ()))
NN = (((1,), (0,)), ((), ()))
TN = (((0,), (0,)), ((), ()))


def split(x):
    hi = x.astype(BF)
    return hi, (x - hi.astype(F32)).astype(BF)


def dot(a, b, dims):
    return lax.dot_general(a, b, dims, preferred_element_type=F32)


def dot3(a, b, dims):
    ah, al = a
    bh, bl = b
    return dot(ah, bh, dims) + (dot(ah, bl, dims) + dot(al, bh, dims))


def gram(a, b):
    return jnp.exp2(gain2 * dot(a, b, NT) - gain2)


def eye(n):
    return (
        lax.broadcasted_iota(jnp.int32, (n, n), 0) == lax.broadcasted_iota(jnp.int32, (n, n), 1)
    ).astype(F32)


def leaf(block):
    groups = LEAF // SUB
    ident = eye(LEAF)
    a = [block[g * SUB:(g + 1) * SUB] for g in range(groups)]
    m = [ident[g * SUB:(g + 1) * SUB] for g in range(groups)]
    sub = lax.broadcasted_iota(jnp.int32, (SUB, LEAF), 0)

    def lane(x, at):
        return jnp.broadcast_to(x[:, at:at + 1], (SUB, LEAF))

    def row(x, at):
        return jnp.broadcast_to(x[at:at + 1, :], (SUB, LEAF))

    for p in range(groups):
        ra, rm = a[p], m[p]
        c = [lane(ra, p * SUB + k) for k in range(SUB)]
        scale, ua, um, uc = [], [], [], []
        for j in range(SUB):
            r = lax.rsqrt(row(c[j], j))
            below = jnp.where(sub > j, c[j] * r, 0.0)
            wa, wm = row(ra, j) * r, row(rm, j) * r
            wc = [row(c[k], j) * r for k in range(j + 1, SUB)]
            scale.append(r)
            ua.append(wa)
            um.append(wm)
            uc.append(wc)
            for k in range(j + 1, SUB):
                c[k] = c[k] - below * wc[k - j - 1]
            ra = jnp.where(sub == j, wa, ra - below * wa)
            rm = jnp.where(sub == j, wm, rm - below * wm)
        a[p], m[p] = ra, rm
        for g in range(p + 1, groups):
            c = [lane(a[g], p * SUB + k) for k in range(SUB)]
            for j in range(SUB):
                l = c[j] * scale[j]
                for k in range(j + 1, SUB):
                    c[k] = c[k] - l * uc[j][k - j - 1]
                a[g] = a[g] - l * ua[j]
                m[g] = m[g] - l * um[j]
    return jnp.concatenate(m, axis=0)


def factor_body(front_ref, hi_ref, lo_ref, work):
    n = front_ref.shape[0]
    blocks = n // LEAF
    f = front_ref[...]
    work[:, 0:n] = gram(f, f) + eye(n)
    work[:, n:2 * n] = eye(n)

    def step(b, carry):
        here = pl.ds(pl.multiple_of(b * LEAF, LEAF), LEAF)
        inverse = leaf(work[here, here])
        for at in range(blocks):
            lo_at, up = at * LEAF, (at + 1) * LEAF

            @pl.when(b == at)
            def _():
                inv = split(inverse)
                if at:
                    work[lo_at:up, n:n + lo_at] = dot3(
                        inv, split(work[lo_at:up, n:n + lo_at]), NN
                    )
                work[lo_at:up, n + lo_at:n + up] = inverse
                if up < n:
                    right = dot3(inv, split(work[lo_at:up, up:n]), NN)
                    rs = split(right)
                    work[up:n, up:n] = work[up:n, up:n] - dot3(rs, rs, TN)
                    ms = split(work[lo_at:up, n:n + up])
                    work[up:n, n:n + up] = work[up:n, n:n + up] - dot3(rs, ms, TN)

        return carry

    lax.fori_loop(0, blocks, step, 0)
    hi, lo = split(work[:, n:2 * n])
    hi_ref[...] = hi
    lo_ref[...] = lo


def factor(front):
    n = front.shape[0]
    shape = jax.ShapeDtypeStruct((n, n), BF)
    return pl.pallas_call(
        factor_body,
        out_shape=(shape, shape),
        in_specs=[pl.BlockSpec(memory_space=pltpu.VMEM)],
        out_specs=(pl.BlockSpec(memory_space=pltpu.VMEM),) * 2,
        scratch_shapes=[pltpu.VMEM((n, 2 * n), F32)],
        cost_estimate=pl.CostEstimate(flops=int(2e10), bytes_accessed=int(5e7), transcendentals=0),
        name="factor",
    )(front)


def exchange_body(
    unit_ref, cols_ref, front_ref, held, own_sem, up_send, up_recv, dn_send, dn_recv, col_send,
    col_recv, front_send, front_recv, keep_sem,
):
    rows = lax.axis_size("row")
    peers = lax.axis_size("col")
    r = lax.axis_index("row")
    c = lax.axis_index("col")
    piece = unit_ref.shape[2]

    barrier = pltpu.get_barrier_semaphore()
    for d in range(1, rows):
        pl.semaphore_signal(
            barrier, inc=1, device_id=(lax.rem(r + d, rows), c),
            device_id_type=pl.DeviceIdType.MESH,
        )
    for d in range(1, peers):
        pl.semaphore_signal(
            barrier, inc=1, device_id=(r, lax.rem(c + d, peers)),
            device_id_type=pl.DeviceIdType.MESH,
        )
    pl.semaphore_wait(barrier, rows + peers - 2)

    own = pltpu.make_async_copy(unit_ref, held.at[r], own_sem)
    own.start()
    own.wait()

    def hop(block, target, send, recv):
        return pltpu.make_async_remote_copy(
            src_ref=held.at[block], dst_ref=held.at[block], send_sem=send, recv_sem=recv,
            device_id=(target, c), device_id_type=pl.DeviceIdType.MESH,
        )

    def up(step):
        return hop(r - step, r + 1, up_send.at[step], up_recv.at[step])

    def down(step):
        return hop(r + step, r - 1, dn_send.at[step], dn_recv.at[step])

    def arrived_up(step):
        return hop(r - 1 - step, r - 1, up_send.at[step], up_recv.at[step])

    def arrived_down(step):
        return hop(r + 1 + step, r + 1, dn_send.at[step], dn_recv.at[step])

    for step in range(rows - 1):
        @pl.when((r + 1 < rows) & (r - step >= 0))
        def _():
            up(step).start()

        @pl.when((r - 1 >= 0) & (r + step < rows))
        def _():
            down(step).start()

        @pl.when(r - 1 - step >= 0)
        def _():
            arrived_up(step).wait_recv()

        @pl.when(r + 1 + step < rows)
        def _():
            arrived_down(step).wait_recv()

    here = pl.ds(pl.multiple_of(c * piece, piece), piece)
    front_src = held.at[0:2, 0, 0]
    front_dst = front_ref.at[:, here]
    copies = []
    for d in range(1, peers):
        peer = lax.rem(c + d, peers)
        copies.append(
            pltpu.make_async_remote_copy(
                src_ref=front_src, dst_ref=front_dst, send_sem=front_send.at[d],
                recv_sem=front_recv.at[d], device_id=(r, peer),
                device_id_type=pl.DeviceIdType.MESH,
            )
        )
        copies.append(
            pltpu.make_async_remote_copy(
                src_ref=held.at[lax.rem(peer, rows), :, peer // rows],
                dst_ref=cols_ref.at[:, here], send_sem=col_send.at[d],
                recv_sem=col_recv.at[d], device_id=(r, peer),
                device_id_type=pl.DeviceIdType.MESH,
            )
        )
    for copy in copies:
        copy.start()
    kept = [
        pltpu.make_async_copy(front_src, front_dst, keep_sem.at[0]),
        pltpu.make_async_copy(
            held.at[lax.rem(c, rows), :, c // rows], cols_ref.at[:, here], keep_sem.at[1]
        ),
    ]
    for copy in kept:
        copy.start()
    for copy in kept:
        copy.wait()
    for copy in copies:
        copy.wait_send()
    for d in range(1, peers):
        peer = lax.rem(c - d + peers, peers)
        there = pl.ds(pl.multiple_of(peer * piece, piece), piece)
        pltpu.make_async_remote_copy(
            src_ref=front_src, dst_ref=front_ref.at[:, there], send_sem=front_send.at[d],
            recv_sem=front_recv.at[d], device_id=(r, peer), device_id_type=pl.DeviceIdType.MESH,
        ).wait_recv()
        pltpu.make_async_remote_copy(
            src_ref=held.at[lax.rem(c, rows), :, c // rows], dst_ref=cols_ref.at[:, there],
            send_sem=col_send.at[d], recv_sem=col_recv.at[d], device_id=(r, peer),
            device_id_type=pl.DeviceIdType.MESH,
        ).wait_recv()
    for step in range(rows - 1):
        @pl.when((r + 1 < rows) & (r - step >= 0))
        def _():
            up(step).wait_send()

        @pl.when((r - 1 >= 0) & (r + step < rows))
        def _():
            down(step).wait_send()


def exchange(unit, row_count, col_count):
    local_tiles, piece, feat = unit.shape
    stride = col_count // row_count
    across = local_tiles // stride
    tile_len = piece * col_count
    dma = pltpu.SemaphoreType.DMA
    anywhere = pl.BlockSpec(memory_space=pl.ANY)
    return pl.pallas_call(
        exchange_body,
        out_shape=(
            jax.ShapeDtypeStruct((across, tile_len, feat), BF),
            jax.ShapeDtypeStruct((2, tile_len, feat), BF),
        ),
        in_specs=[anywhere],
        out_specs=(anywhere, anywhere),
        scratch_shapes=[
            pltpu.VMEM((row_count, across, stride, piece, feat), BF),
            dma, dma((row_count,)), dma((row_count,)), dma((row_count,)), dma((row_count,)),
            dma((col_count,)), dma((col_count,)), dma((col_count,)), dma((col_count,)), dma((2,)),
        ],
        compiler_params=pltpu.CompilerParams(collective_id=0, has_side_effects=True),
        cost_estimate=pl.CostEstimate(flops=int(2e10), bytes_accessed=int(5e7), transcendentals=0),
        name="exchange",
    )(unit.reshape(across, stride, piece, feat))


def panel_of(points, tile_id, front, hi_ref, lo_ref, tile_len):
    n = front.shape[0]
    values = gram(points, front)
    at = lax.broadcasted_iota(jnp.int32, values.shape, 0) + tile_id * tile_len
    values = values + (at == lax.broadcasted_iota(jnp.int32, values.shape, 1)).astype(F32)
    hi, lo = split(values)
    t = tile_len
    first = dot3((hi[:, :t], lo[:, :t]), (hi_ref[:t, :t], lo_ref[:t, :t]), NT)
    second = dot3((hi, lo), (hi_ref[t:, :], lo_ref[t:, :]), NT)
    return jnp.concatenate([first, second], axis=1)


def schur_body(ids, rows_ref, cols_ref, front_ref, hi_ref, lo_ref, out_ref, panel_ref, q_ref):
    tile_len = rows_ref.shape[0]
    across = cols_ref.shape[0] // tile_len
    own_row, row_count, own_col, col_count = ids[0], ids[1], ids[2], ids[3]
    a = pl.program_id(0)
    chunks = across * tile_len // LEAF

    @pl.when(a == 0)
    def _():
        def one(b, carry):
            here = pl.ds(pl.multiple_of(b * tile_len, tile_len), tile_len)
            hi, lo = split(
                panel_of(
                    cols_ref[here, :], b * col_count + own_col, front_ref[...], hi_ref, lo_ref,
                    tile_len,
                )
            )
            q_ref[here, :] = jnp.concatenate([hi, lo[:, :LEAF], hi[:, :LEAF]], axis=1)
            return carry

        lax.fori_loop(0, across, one, 0)

    tile_id = a * row_count + own_row
    points = rows_ref[...]
    panel = panel_of(points, tile_id, front_ref[...], hi_ref, lo_ref, tile_len)
    panel_ref[...] = panel
    hi, lo = split(panel)
    p = jnp.concatenate([hi, hi[:, :LEAF], lo[:, :LEAF]], axis=1)
    per = tile_len // LEAF
    for b in range(across):
        here = slice(b * tile_len, (b + 1) * tile_len)
        s = gram(points, cols_ref[here, :]) - dot(p, q_ref[here, :], NT)
        for k in range(per):
            out_ref[pl.ds(b * per + k, tile_len, stride=chunks), :] = s[:, k * LEAF:(k + 1) * LEAF]

        @pl.when(tile_id == b * col_count + own_col)
        def _():
            ident = eye(tile_len)
            for k in range(per):
                at = pl.ds(b * per + k, tile_len, stride=chunks)
                out_ref[at, :] = out_ref[at, :] + ident[:, k * LEAF:(k + 1) * LEAF]


def schur(ids, row_points, col_points, front, hi, lo, tile_len):
    rows, feat = row_points.shape
    cols = col_points.shape[0]
    n = front.shape[0]
    chunks = cols // LEAF

    def whole(shape):
        return pl.BlockSpec(shape, lambda a, ids: (0, 0))

    return pl.pallas_call(
        schur_body,
        out_shape=(
            jax.ShapeDtypeStruct((rows * chunks, LEAF), F32),
            jax.ShapeDtypeStruct((rows, n), F32),
        ),
        grid_spec=pltpu.PrefetchScalarGridSpec(
            num_scalar_prefetch=1,
            grid=(rows // tile_len,),
            in_specs=[
                pl.BlockSpec((tile_len, feat), lambda a, ids: (a, 0)),
                whole((cols, feat)),
                whole((n, feat)),
                whole((n, n)),
                whole((n, n)),
            ],
            out_specs=(
                pl.BlockSpec((tile_len * chunks, LEAF), lambda a, ids: (a, 0)),
                pl.BlockSpec((tile_len, n), lambda a, ids: (a, 0)),
            ),
            scratch_shapes=[pltpu.VMEM((cols, n + 2 * LEAF), BF)],
        ),
        compiler_params=pltpu.CompilerParams(dimension_semantics=("arbitrary",)),
        name="schur",
    )(ids, row_points, col_points, front, hi, lo)


def per_device(features):
    row_count = lax.axis_size("row")
    col_count = lax.axis_size("col")
    own_row = lax.axis_index("row")
    own_col = lax.axis_index("col")
    floated = features.astype(F32)
    unit = (
        floated * lax.rsqrt(jnp.sum(floated * floated, axis=-1, keepdims=True) + epsilon)
    ).astype(BF)
    local_tiles, _, piece, feat = unit.shape
    tile_len = piece * col_count
    gathered = lax.all_gather(unit, "col", axis=2, tiled=True)
    cols, leading = exchange(unit[:, 0], row_count, col_count)
    front = leading.reshape(2 * tile_len, feat)
    col_points = cols.reshape(-1, feat)
    hi, lo = factor(front)
    row_points = gathered.reshape(-1, feat)
    ids = jnp.stack(
        [own_row, jnp.int32(row_count), own_col, jnp.int32(col_count)]
    ).astype(jnp.int32)
    big, panels = schur(ids, row_points, col_points, front, hi, lo, tile_len)
    across = col_points.shape[0] // tile_len
    return (
        big.reshape(local_tiles, 1, tile_len, across, 1, tile_len),
        panels.reshape(local_tiles, 1, tile_len, 2 * tile_len),
    )


def solution(mesh):
    return jax.shard_map(
        per_device,
        mesh=mesh,
        in_specs=(P(None, "row", "col", None),),
        out_specs=(P(None, "row", None, None, "col", None), P(None, "row", None, None)),
        check_vma=False,
    )
```

```python
import math

import jax
import jax.numpy as jnp
from jax import lax
from jax.experimental import pallas as pl
from jax.experimental.pallas import tpu as pltpu
from jax.sharding import PartitionSpec as P

kernel_gain = 2.0
epsilon = 1e-06
LEAF = 128
SUB = 8
gain2 = kernel_gain / math.log(2.0)
BF = jnp.bfloat16
F32 = jnp.float32
NT = (((1,), (1,)), ((), ()))
NN = (((1,), (0,)), ((), ()))
TN = (((0,), (0,)), ((), ()))


def split(x):
    hi = x.astype(BF)
    return hi, (x - hi.astype(F32)).astype(BF)


def dot(a, b, dims):
    return lax.dot_general(a, b, dims, preferred_element_type=F32)


def dot3(a, b, dims):
    ah, al = a
    bh, bl = b
    return dot(ah, bh, dims) + (dot(ah, bl, dims) + dot(al, bh, dims))


def gram(a, b):
    return jnp.exp2(gain2 * dot(a, b, NT) - gain2)


def eye(n):
    return (
        lax.broadcasted_iota(jnp.int32, (n, n), 0) == lax.broadcasted_iota(jnp.int32, (n, n), 1)
    ).astype(F32)


def leaf(block):
    groups = LEAF // SUB
    ident = eye(LEAF)
    a = [block[g * SUB:(g + 1) * SUB] for g in range(groups)]
    m = [ident[g * SUB:(g + 1) * SUB] for g in range(groups)]
    sub = lax.broadcasted_iota(jnp.int32, (SUB, LEAF), 0)

    def lane(x, at):
        return jnp.broadcast_to(x[:, at:at + 1], (SUB, LEAF))

    def row(x, at):
        return jnp.broadcast_to(x[at:at + 1, :], (SUB, LEAF))

    for p in range(groups):
        ra, rm = a[p], m[p]
        c = [lane(ra, p * SUB + k) for k in range(SUB)]
        scale, ua, um, uc = [], [], [], []
        for j in range(SUB):
            r = lax.rsqrt(row(c[j], j))
            below = jnp.where(sub > j, c[j] * r, 0.0)
            wa, wm = row(ra, j) * r, row(rm, j) * r
            wc = [row(c[k], j) * r for k in range(j + 1, SUB)]
            scale.append(r)
            ua.append(wa)
            um.append(wm)
            uc.append(wc)
            for k in range(j + 1, SUB):
                c[k] = c[k] - below * wc[k - j - 1]
            ra = jnp.where(sub == j, wa, ra - below * wa)
            rm = jnp.where(sub == j, wm, rm - below * wm)
        a[p], m[p] = ra, rm
        for g in range(p + 1, groups):
            c = [lane(a[g], p * SUB + k) for k in range(SUB)]
            for j in range(SUB):
                l = c[j] * scale[j]
                for k in range(j + 1, SUB):
                    c[k] = c[k] - l * uc[j][k - j - 1]
                a[g] = a[g] - l * ua[j]
                m[g] = m[g] - l * um[j]
    return jnp.concatenate(m, axis=0)


def factor_body(front_ref, hi_ref, lo_ref, work):
    n = front_ref.shape[0]
    blocks = n // LEAF
    f = front_ref[...]
    work[:, 0:n] = gram(f, f) + eye(n)
    work[:, n:2 * n] = eye(n)

    def step(b, carry):
        here = pl.ds(pl.multiple_of(b * LEAF, LEAF), LEAF)
        inverse = leaf(work[here, here])
        for at in range(blocks):
            lo_at, up = at * LEAF, (at + 1) * LEAF

            @pl.when(b == at)
            def _():
                inv = split(inverse)
                if at:
                    work[lo_at:up, n:n + lo_at] = dot3(
                        inv, split(work[lo_at:up, n:n + lo_at]), NN
                    )
                work[lo_at:up, n + lo_at:n + up] = inverse
                if up < n:
                    right = dot3(inv, split(work[lo_at:up, up:n]), NN)
                    rs = split(right)
                    work[up:n, up:n] = work[up:n, up:n] - dot3(rs, rs, TN)
                    ms = split(work[lo_at:up, n:n + up])
                    work[up:n, n:n + up] = work[up:n, n:n + up] - dot3(rs, ms, TN)

        return carry

    lax.fori_loop(0, blocks, step, 0)
    hi, lo = split(work[:, n:2 * n])
    hi_ref[...] = hi
    lo_ref[...] = lo


def factor(front):
    n = front.shape[0]
    shape = jax.ShapeDtypeStruct((n, n), BF)
    return pl.pallas_call(
        factor_body,
        out_shape=(shape, shape),
        in_specs=[pl.BlockSpec(memory_space=pltpu.VMEM)],
        out_specs=(pl.BlockSpec(memory_space=pltpu.VMEM),) * 2,
        scratch_shapes=[pltpu.VMEM((n, 2 * n), F32)],
        cost_estimate=pl.CostEstimate(flops=int(2e10), bytes_accessed=int(5e7), transcendentals=0),
        name="factor",
    )(front)


def exchange_body(
    unit_ref, cols_ref, front_ref, held, own_sem, up_send, up_recv, dn_send, dn_recv, col_send,
    col_recv, front_send, front_recv, keep_sem,
):
    rows = lax.axis_size("row")
    peers = lax.axis_size("col")
    r = lax.axis_index("row")
    c = lax.axis_index("col")
    piece = unit_ref.shape[2]

    barrier = pltpu.get_barrier_semaphore()
    for d in range(1, rows):
        pl.semaphore_signal(
            barrier, inc=1, device_id=(lax.rem(r + d, rows), c),
            device_id_type=pl.DeviceIdType.MESH,
        )
    for d in range(1, peers):
        pl.semaphore_signal(
            barrier, inc=1, device_id=(r, lax.rem(c + d, peers)),
            device_id_type=pl.DeviceIdType.MESH,
        )
    pl.semaphore_wait(barrier, rows + peers - 2)

    own = pltpu.make_async_copy(unit_ref, held.at[r], own_sem)
    own.start()
    own.wait()

    def hop(block, target, send, recv):
        return pltpu.make_async_remote_copy(
            src_ref=held.at[block], dst_ref=held.at[block], send_sem=send, recv_sem=recv,
            device_id=(target, c), device_id_type=pl.DeviceIdType.MESH,
        )

    def up(step):
        return hop(r - step, r + 1, up_send.at[step], up_recv.at[step])

    def down(step):
        return hop(r + step, r - 1, dn_send.at[step], dn_recv.at[step])

    def arrived_up(step):
        return hop(r - 1 - step, r - 1, up_send.at[step], up_recv.at[step])

    def arrived_down(step):
        return hop(r + 1 + step, r + 1, dn_send.at[step], dn_recv.at[step])

    for step in range(rows - 1):
        @pl.when((r + 1 < rows) & (r - step >= 0))
        def _():
            up(step).start()

        @pl.when((r - 1 >= 0) & (r + step < rows))
        def _():
            down(step).start()

        @pl.when(r - 1 - step >= 0)
        def _():
            arrived_up(step).wait_recv()

        @pl.when(r + 1 + step < rows)
        def _():
            arrived_down(step).wait_recv()

    here = pl.ds(pl.multiple_of(c * piece, piece), piece)
    front_src = held.at[0:2, 0, 0]
    front_dst = front_ref.at[:, here]
    copies = []
    for d in range(1, peers):
        peer = lax.rem(c + d, peers)
        copies.append(
            pltpu.make_async_remote_copy(
                src_ref=front_src, dst_ref=front_dst, send_sem=front_send.at[d],
                recv_sem=front_recv.at[d], device_id=(r, peer),
                device_id_type=pl.DeviceIdType.MESH,
            )
        )
        copies.append(
            pltpu.make_async_remote_copy(
                src_ref=held.at[lax.rem(peer, rows), :, peer // rows],
                dst_ref=cols_ref.at[:, here], send_sem=col_send.at[d],
                recv_sem=col_recv.at[d], device_id=(r, peer),
                device_id_type=pl.DeviceIdType.MESH,
            )
        )
    for copy in copies:
        copy.start()
    kept = [
        pltpu.make_async_copy(front_src, front_dst, keep_sem.at[0]),
        pltpu.make_async_copy(
            held.at[lax.rem(c, rows), :, c // rows], cols_ref.at[:, here], keep_sem.at[1]
        ),
    ]
    for copy in kept:
        copy.start()
    for copy in kept:
        copy.wait()
    for copy in copies:
        copy.wait_send()
    for d in range(1, peers):
        peer = lax.rem(c - d + peers, peers)
        there = pl.ds(pl.multiple_of(peer * piece, piece), piece)
        pltpu.make_async_remote_copy(
            src_ref=front_src, dst_ref=front_ref.at[:, there], send_sem=front_send.at[d],
            recv_sem=front_recv.at[d], device_id=(r, peer), device_id_type=pl.DeviceIdType.MESH,
        ).wait_recv()
        pltpu.make_async_remote_copy(
            src_ref=held.at[lax.rem(c, rows), :, c // rows], dst_ref=cols_ref.at[:, there],
            send_sem=col_send.at[d], recv_sem=col_recv.at[d], device_id=(r, peer),
            device_id_type=pl.DeviceIdType.MESH,
        ).wait_recv()
    for step in range(rows - 1):
        @pl.when((r + 1 < rows) & (r - step >= 0))
        def _():
            up(step).wait_send()

        @pl.when((r - 1 >= 0) & (r + step < rows))
        def _():
            down(step).wait_send()


def exchange(unit, row_count, col_count):
    local_tiles, piece, feat = unit.shape
    stride = col_count // row_count
    across = local_tiles // stride
    tile_len = piece * col_count
    dma = pltpu.SemaphoreType.DMA
    anywhere = pl.BlockSpec(memory_space=pl.ANY)
    return pl.pallas_call(
        exchange_body,
        out_shape=(
            jax.ShapeDtypeStruct((across, tile_len, feat), BF),
            jax.ShapeDtypeStruct((2, tile_len, feat), BF),
        ),
        in_specs=[anywhere],
        out_specs=(anywhere, anywhere),
        scratch_shapes=[
            pltpu.VMEM((row_count, across, stride, piece, feat), BF),
            dma, dma((row_count,)), dma((row_count,)), dma((row_count,)), dma((row_count,)),
            dma((col_count,)), dma((col_count,)), dma((col_count,)), dma((col_count,)), dma((2,)),
        ],
        compiler_params=pltpu.CompilerParams(collective_id=0, has_side_effects=True),
        cost_estimate=pl.CostEstimate(flops=int(2e10), bytes_accessed=int(5e7), transcendentals=0),
        name="exchange",
    )(unit.reshape(across, stride, piece, feat))


def panel_of(points, tile_id, front, hi_ref, lo_ref, tile_len):
    n = front.shape[0]
    values = gram(points, front)
    at = lax.broadcasted_iota(jnp.int32, values.shape, 0) + tile_id * tile_len
    values = values + (at == lax.broadcasted_iota(jnp.int32, values.shape, 1)).astype(F32)
    hi, lo = split(values)
    t = tile_len
    first = dot3((hi[:, :t], lo[:, :t]), (hi_ref[:t, :t], lo_ref[:t, :t]), NT)
    second = dot3((hi, lo), (hi_ref[t:, :], lo_ref[t:, :]), NT)
    return jnp.concatenate([first, second], axis=1)


def schur_body(ids, rows_ref, cols_ref, front_ref, hi_ref, lo_ref, out_ref, panel_ref, q_ref):
    tile_len = rows_ref.shape[0]
    across = cols_ref.shape[0] // tile_len
    own_row, row_count, own_col, col_count = ids[0], ids[1], ids[2], ids[3]
    a = pl.program_id(0)
    chunks = across * tile_len // LEAF

    @pl.when(a == 0)
    def _():
        def one(b, carry):
            here = pl.ds(pl.multiple_of(b * tile_len, tile_len), tile_len)
            hi, lo = split(
                panel_of(
                    cols_ref[here, :], b * col_count + own_col, front_ref[...], hi_ref, lo_ref,
                    tile_len,
                )
            )
            q_ref[here, :] = jnp.concatenate([hi, lo[:, :LEAF], hi[:, :LEAF]], axis=1)
            return carry

        lax.fori_loop(0, across, one, 0)

    tile_id = a * row_count + own_row
    points = rows_ref[...]
    panel = panel_of(points, tile_id, front_ref[...], hi_ref, lo_ref, tile_len)
    panel_ref[...] = panel
    hi, lo = split(panel)
    p = jnp.concatenate([hi, hi[:, :LEAF], lo[:, :LEAF]], axis=1)
    per = tile_len // LEAF
    s = gram(points, cols_ref[...]) - dot(p, q_ref[...], NT)
    for k in range(chunks):
        out_ref[pl.ds(k, tile_len, stride=chunks), :] = s[:, k * LEAF:(k + 1) * LEAF]

    for b in range(across):
        @pl.when(tile_id == b * col_count + own_col)
        def _():
            ident = eye(tile_len)
            for k in range(per):
                at = pl.ds(b * per + k, tile_len, stride=chunks)
                out_ref[at, :] = out_ref[at, :] + ident[:, k * LEAF:(k + 1) * LEAF]


def schur(ids, row_points, col_points, front, hi, lo, tile_len):
    rows, feat = row_points.shape
    cols = col_points.shape[0]
    n = front.shape[0]
    chunks = cols // LEAF

    def whole(shape):
        return pl.BlockSpec(shape, lambda a, ids: (0, 0))

    return pl.pallas_call(
        schur_body,
        out_shape=(
            jax.ShapeDtypeStruct((rows * chunks, LEAF), F32),
            jax.ShapeDtypeStruct((rows, n), F32),
        ),
        grid_spec=pltpu.PrefetchScalarGridSpec(
            num_scalar_prefetch=1,
            grid=(rows // tile_len,),
            in_specs=[
                pl.BlockSpec((tile_len, feat), lambda a, ids: (a, 0)),
                whole((cols, feat)),
                whole((n, feat)),
                whole((n, n)),
                whole((n, n)),
            ],
            out_specs=(
                pl.BlockSpec((tile_len * chunks, LEAF), lambda a, ids: (a, 0)),
                pl.BlockSpec((tile_len, n), lambda a, ids: (a, 0)),
            ),
            scratch_shapes=[pltpu.VMEM((cols, n + 2 * LEAF), BF)],
        ),
        compiler_params=pltpu.CompilerParams(dimension_semantics=("arbitrary",)),
        name="schur",
    )(ids, row_points, col_points, front, hi, lo)


def per_device(features):
    row_count = lax.axis_size("row")
    col_count = lax.axis_size("col")
    own_row = lax.axis_index("row")
    own_col = lax.axis_index("col")
    floated = features.astype(F32)
    unit = (
        floated * lax.rsqrt(jnp.sum(floated * floated, axis=-1, keepdims=True) + epsilon)
    ).astype(BF)
    local_tiles, _, piece, feat = unit.shape
    tile_len = piece * col_count
    gathered = lax.all_gather(unit, "col", axis=2, tiled=True)
    cols, leading = exchange(unit[:, 0], row_count, col_count)
    front = leading.reshape(2 * tile_len, feat)
    col_points = cols.reshape(-1, feat)
    hi, lo = factor(front)
    row_points = gathered.reshape(-1, feat)
    ids = jnp.stack(
        [own_row, jnp.int32(row_count), own_col, jnp.int32(col_count)]
    ).astype(jnp.int32)
    big, panels = schur(ids, row_points, col_points, front, hi, lo, tile_len)
    across = col_points.shape[0] // tile_len
    return (
        big.reshape(local_tiles, 1, tile_len, across, 1, tile_len),
        panels.reshape(local_tiles, 1, tile_len, 2 * tile_len),
    )


def solution(mesh):
    return jax.shard_map(
        per_device,
        mesh=mesh,
        in_specs=(P(None, "row", "col", None),),
        out_specs=(P(None, "row", None, None, "col", None), P(None, "row", None, None)),
        check_vma=False,
    )
```

```python
import math

import jax
import jax.numpy as jnp
from jax import lax
from jax.experimental import pallas as pl
from jax.experimental.pallas import tpu as pltpu
from jax.sharding import PartitionSpec as P

kernel_gain = 2.0
epsilon = 1e-06
LEAF = 128
SUB = 8
gain2 = kernel_gain / math.log(2.0)
BF = jnp.bfloat16
F32 = jnp.float32
NT = (((1,), (1,)), ((), ()))
NN = (((1,), (0,)), ((), ()))
TN = (((0,), (0,)), ((), ()))


def split(x):
    hi = x.astype(BF)
    return hi, (x - hi.astype(F32)).astype(BF)


def dot(a, b, dims):
    return lax.dot_general(a, b, dims, preferred_element_type=F32)


def dot3(a, b, dims):
    ah, al = a
    bh, bl = b
    return dot(ah, bh, dims) + (dot(ah, bl, dims) + dot(al, bh, dims))


def gram(a, b):
    return jnp.exp2(gain2 * dot(a, b, NT) - gain2)


def eye(n):
    return (
        lax.broadcasted_iota(jnp.int32, (n, n), 0) == lax.broadcasted_iota(jnp.int32, (n, n), 1)
    ).astype(F32)


def leaf(block):
    groups = LEAF // SUB
    ident = eye(LEAF)
    a = [block[g * SUB:(g + 1) * SUB] for g in range(groups)]
    m = [ident[g * SUB:(g + 1) * SUB] for g in range(groups)]
    sub = lax.broadcasted_iota(jnp.int32, (SUB, LEAF), 0)

    def lane(x, at):
        return jnp.broadcast_to(x[:, at:at + 1], (SUB, LEAF))

    def row(x, at):
        return jnp.broadcast_to(x[at:at + 1, :], (SUB, LEAF))

    for p in range(groups):
        ra, rm = a[p], m[p]
        c = [lane(ra, p * SUB + k) for k in range(SUB)]
        scale, ua, um, uc = [], [], [], []
        for j in range(SUB):
            r = lax.rsqrt(row(c[j], j))
            below = jnp.where(sub > j, c[j] * r, 0.0)
            wa, wm = row(ra, j) * r, row(rm, j) * r
            wc = [row(c[k], j) * r for k in range(j + 1, SUB)]
            scale.append(r)
            ua.append(wa)
            um.append(wm)
            uc.append(wc)
            for k in range(j + 1, SUB):
                c[k] = c[k] - below * wc[k - j - 1]
            ra = jnp.where(sub == j, wa, ra - below * wa)
            rm = jnp.where(sub == j, wm, rm - below * wm)
        a[p], m[p] = ra, rm
        for g in range(p + 1, groups):
            c = [lane(a[g], p * SUB + k) for k in range(SUB)]
            for j in range(SUB):
                l = c[j] * scale[j]
                for k in range(j + 1, SUB):
                    c[k] = c[k] - l * uc[j][k - j - 1]
                a[g] = a[g] - l * ua[j]
                m[g] = m[g] - l * um[j]
    return jnp.concatenate(m, axis=0)


def factor_body(front_ref, hi_ref, lo_ref, work):
    n = front_ref.shape[0]
    blocks = n // LEAF
    f = front_ref[...]
    work[:, 0:n] = gram(f, f) + eye(n)
    work[:, n:2 * n] = eye(n)

    def step(b, carry):
        here = pl.ds(pl.multiple_of(b * LEAF, LEAF), LEAF)
        inverse = leaf(work[here, here])
        for at in range(blocks):
            lo_at, up = at * LEAF, (at + 1) * LEAF

            @pl.when(b == at)
            def _():
                inv = split(inverse)
                if at:
                    work[lo_at:up, n:n + lo_at] = dot3(
                        inv, split(work[lo_at:up, n:n + lo_at]), NN
                    )
                work[lo_at:up, n + lo_at:n + up] = inverse
                if up < n:
                    right = dot3(inv, split(work[lo_at:up, up:n]), NN)
                    rs = split(right)
                    work[up:n, up:n] = work[up:n, up:n] - dot3(rs, rs, TN)
                    ms = split(work[lo_at:up, n:n + up])
                    work[up:n, n:n + up] = work[up:n, n:n + up] - dot3(rs, ms, TN)

        return carry

    lax.fori_loop(0, blocks, step, 0)
    hi, lo = split(work[:, n:2 * n])
    hi_ref[...] = hi
    lo_ref[...] = lo


def factor(front):
    n = front.shape[0]
    shape = jax.ShapeDtypeStruct((n, n), BF)
    return pl.pallas_call(
        factor_body,
        out_shape=(shape, shape),
        in_specs=[pl.BlockSpec(memory_space=pltpu.VMEM)],
        out_specs=(pl.BlockSpec(memory_space=pltpu.VMEM),) * 2,
        scratch_shapes=[pltpu.VMEM((n, 2 * n), F32)],
        cost_estimate=pl.CostEstimate(flops=int(2e10), bytes_accessed=int(5e7), transcendentals=0),
        name="factor",
    )(front)


def exchange_body(
    unit_ref, cols_ref, front_ref, held, own_sem, up_send, up_recv, dn_send, dn_recv, col_send,
    col_recv, front_send, front_recv, keep_sem,
):
    rows = lax.axis_size("row")
    peers = lax.axis_size("col")
    r = lax.axis_index("row")
    c = lax.axis_index("col")
    piece = unit_ref.shape[2]

    barrier = pltpu.get_barrier_semaphore()
    for d in range(1, rows):
        pl.semaphore_signal(
            barrier, inc=1, device_id=(lax.rem(r + d, rows), c),
            device_id_type=pl.DeviceIdType.MESH,
        )
    for d in range(1, peers):
        pl.semaphore_signal(
            barrier, inc=1, device_id=(r, lax.rem(c + d, peers)),
            device_id_type=pl.DeviceIdType.MESH,
        )
    pl.semaphore_wait(barrier, rows + peers - 2)

    own = pltpu.make_async_copy(unit_ref, held.at[r], own_sem)
    own.start()
    own.wait()

    def hop(block, target, send, recv):
        return pltpu.make_async_remote_copy(
            src_ref=held.at[block], dst_ref=held.at[block], send_sem=send, recv_sem=recv,
            device_id=(target, c), device_id_type=pl.DeviceIdType.MESH,
        )

    def up(step):
        return hop(r - step, r + 1, up_send.at[step], up_recv.at[step])

    def down(step):
        return hop(r + step, r - 1, dn_send.at[step], dn_recv.at[step])

    def arrived_up(step):
        return hop(r - 1 - step, r - 1, up_send.at[step], up_recv.at[step])

    def arrived_down(step):
        return hop(r + 1 + step, r + 1, dn_send.at[step], dn_recv.at[step])

    here = pl.ds(pl.multiple_of(c * piece, piece), piece)

    def hand_out(block):
        for turn in range(unit_ref.shape[1]):
            peer = block + turn * rows
            away = lax.rem(peer - c + peers, peers)

            @pl.when(peer != c)
            def _():
                pltpu.make_async_remote_copy(
                    src_ref=held.at[block, :, turn], dst_ref=cols_ref.at[:, here],
                    send_sem=col_send.at[away], recv_sem=col_recv.at[away],
                    device_id=(r, peer), device_id_type=pl.DeviceIdType.MESH,
                ).start()

    for step in range(rows - 1):
        @pl.when((r + 1 < rows) & (r - step >= 0))
        def _():
            up(step).start()

        @pl.when((r - 1 >= 0) & (r + step < rows))
        def _():
            down(step).start()

        if step == 0:
            hand_out(r)

        @pl.when(r - 1 - step >= 0)
        def _():
            arrived_up(step).wait_recv()
            hand_out(r - 1 - step)

        @pl.when(r + 1 + step < rows)
        def _():
            arrived_down(step).wait_recv()
            hand_out(r + 1 + step)

    front_src = held.at[0:2, 0, 0]
    front_dst = front_ref.at[:, here]
    copies = []
    for d in range(1, peers):
        peer = lax.rem(c + d, peers)
        copies.append(
            pltpu.make_async_remote_copy(
                src_ref=front_src, dst_ref=front_dst, send_sem=front_send.at[d],
                recv_sem=front_recv.at[d], device_id=(r, peer),
                device_id_type=pl.DeviceIdType.MESH,
            )
        )
        copies.append(
            pltpu.make_async_remote_copy(
                src_ref=held.at[lax.rem(peer, rows), :, peer // rows],
                dst_ref=cols_ref.at[:, here], send_sem=col_send.at[d],
                recv_sem=col_recv.at[d], device_id=(r, peer),
                device_id_type=pl.DeviceIdType.MESH,
            )
        )
    for copy in copies[::2]:
        copy.start()
    kept = [
        pltpu.make_async_copy(front_src, front_dst, keep_sem.at[0]),
        pltpu.make_async_copy(
            held.at[lax.rem(c, rows), :, c // rows], cols_ref.at[:, here], keep_sem.at[1]
        ),
    ]
    for copy in kept:
        copy.start()
    for copy in kept:
        copy.wait()
    for copy in copies:
        copy.wait_send()
    for d in range(1, peers):
        peer = lax.rem(c - d + peers, peers)
        there = pl.ds(pl.multiple_of(peer * piece, piece), piece)
        pltpu.make_async_remote_copy(
            src_ref=front_src, dst_ref=front_ref.at[:, there], send_sem=front_send.at[d],
            recv_sem=front_recv.at[d], device_id=(r, peer), device_id_type=pl.DeviceIdType.MESH,
        ).wait_recv()
        pltpu.make_async_remote_copy(
            src_ref=held.at[lax.rem(c, rows), :, c // rows], dst_ref=cols_ref.at[:, there],
            send_sem=col_send.at[d], recv_sem=col_recv.at[d], device_id=(r, peer),
            device_id_type=pl.DeviceIdType.MESH,
        ).wait_recv()
    for step in range(rows - 1):
        @pl.when((r + 1 < rows) & (r - step >= 0))
        def _():
            up(step).wait_send()

        @pl.when((r - 1 >= 0) & (r + step < rows))
        def _():
            down(step).wait_send()


def exchange(unit, row_count, col_count):
    local_tiles, piece, feat = unit.shape
    stride = col_count // row_count
    across = local_tiles // stride
    tile_len = piece * col_count
    dma = pltpu.SemaphoreType.DMA
    anywhere = pl.BlockSpec(memory_space=pl.ANY)
    return pl.pallas_call(
        exchange_body,
        out_shape=(
            jax.ShapeDtypeStruct((across, tile_len, feat), BF),
            jax.ShapeDtypeStruct((2, tile_len, feat), BF),
        ),
        in_specs=[anywhere],
        out_specs=(anywhere, anywhere),
        scratch_shapes=[
            pltpu.VMEM((row_count, across, stride, piece, feat), BF),
            dma, dma((row_count,)), dma((row_count,)), dma((row_count,)), dma((row_count,)),
            dma((col_count,)), dma((col_count,)), dma((col_count,)), dma((col_count,)), dma((2,)),
        ],
        compiler_params=pltpu.CompilerParams(collective_id=0, has_side_effects=True),
        cost_estimate=pl.CostEstimate(flops=int(2e10), bytes_accessed=int(5e7), transcendentals=0),
        name="exchange",
    )(unit.reshape(across, stride, piece, feat))


def panel_of(points, tile_id, front, hi_ref, lo_ref, tile_len):
    n = front.shape[0]
    values = gram(points, front)
    at = lax.broadcasted_iota(jnp.int32, values.shape, 0) + tile_id * tile_len
    values = values + (at == lax.broadcasted_iota(jnp.int32, values.shape, 1)).astype(F32)
    hi, lo = split(values)
    t = tile_len
    first = dot3((hi[:, :t], lo[:, :t]), (hi_ref[:t, :t], lo_ref[:t, :t]), NT)
    second = dot3((hi, lo), (hi_ref[t:, :], lo_ref[t:, :]), NT)
    return jnp.concatenate([first, second], axis=1)


def schur_body(ids, rows_ref, cols_ref, front_ref, hi_ref, lo_ref, out_ref, panel_ref, q_ref):
    tile_len = rows_ref.shape[0]
    across = cols_ref.shape[0] // tile_len
    own_row, row_count, own_col, col_count = ids[0], ids[1], ids[2], ids[3]
    a = pl.program_id(0)
    chunks = across * tile_len // LEAF

    @pl.when(a == 0)
    def _():
        def one(b, carry):
            here = pl.ds(pl.multiple_of(b * tile_len, tile_len), tile_len)
            hi, lo = split(
                panel_of(
                    cols_ref[here, :], b * col_count + own_col, front_ref[...], hi_ref, lo_ref,
                    tile_len,
                )
            )
            q_ref[here, :] = jnp.concatenate([hi, lo[:, :LEAF], hi[:, :LEAF]], axis=1)
            return carry

        lax.fori_loop(0, across, one, 0, unroll=True)

    tile_id = a * row_count + own_row
    points = rows_ref[...]
    panel = panel_of(points, tile_id, front_ref[...], hi_ref, lo_ref, tile_len)
    panel_ref[...] = panel
    hi, lo = split(panel)
    p = jnp.concatenate([hi, hi[:, :LEAF], lo[:, :LEAF]], axis=1)
    per = tile_len // LEAF
    s = gram(points, cols_ref[...]) - dot(p, q_ref[...], NT)
    for k in range(chunks):
        out_ref[pl.ds(k, tile_len, stride=chunks), :] = s[:, k * LEAF:(k + 1) * LEAF]

    for b in range(across):
        @pl.when(tile_id == b * col_count + own_col)
        def _():
            ident = eye(tile_len)
            for k in range(per):
                at = pl.ds(b * per + k, tile_len, stride=chunks)
                out_ref[at, :] = out_ref[at, :] + ident[:, k * LEAF:(k + 1) * LEAF]


def schur(ids, row_points, col_points, front, hi, lo, tile_len):
    rows, feat = row_points.shape
    cols = col_points.shape[0]
    n = front.shape[0]
    chunks = cols // LEAF

    def whole(shape):
        return pl.BlockSpec(shape, lambda a, ids: (0, 0))

    return pl.pallas_call(
        schur_body,
        out_shape=(
            jax.ShapeDtypeStruct((rows * chunks, LEAF), F32),
            jax.ShapeDtypeStruct((rows, n), F32),
        ),
        grid_spec=pltpu.PrefetchScalarGridSpec(
            num_scalar_prefetch=1,
            grid=(rows // tile_len,),
            in_specs=[
                pl.BlockSpec((tile_len, feat), lambda a, ids: (a, 0)),
                whole((cols, feat)),
                whole((n, feat)),
                whole((n, n)),
                whole((n, n)),
            ],
            out_specs=(
                pl.BlockSpec((tile_len * chunks, LEAF), lambda a, ids: (a, 0)),
                pl.BlockSpec((tile_len, n), lambda a, ids: (a, 0)),
            ),
            scratch_shapes=[pltpu.VMEM((cols, n + 2 * LEAF), BF)],
        ),
        compiler_params=pltpu.CompilerParams(dimension_semantics=("arbitrary",)),
        name="schur",
    )(ids, row_points, col_points, front, hi, lo)


def per_device(features):
    row_count = lax.axis_size("row")
    col_count = lax.axis_size("col")
    own_row = lax.axis_index("row")
    own_col = lax.axis_index("col")
    floated = features.astype(F32)
    unit = (
        floated * lax.rsqrt(jnp.sum(floated * floated, axis=-1, keepdims=True) + epsilon)
    ).astype(BF)
    local_tiles, _, piece, feat = unit.shape
    tile_len = piece * col_count
    gathered = lax.all_gather(unit, "col", axis=2, tiled=True)
    cols, leading = exchange(unit[:, 0], row_count, col_count)
    front = leading.reshape(2 * tile_len, feat)
    col_points = cols.reshape(-1, feat)
    hi, lo = factor(front)
    row_points = gathered.reshape(-1, feat)
    ids = jnp.stack(
        [own_row, jnp.int32(row_count), own_col, jnp.int32(col_count)]
    ).astype(jnp.int32)
    big, panels = schur(ids, row_points, col_points, front, hi, lo, tile_len)
    across = col_points.shape[0] // tile_len
    return (
        big.reshape(local_tiles, 1, tile_len, across, 1, tile_len),
        panels.reshape(local_tiles, 1, tile_len, 2 * tile_len),
    )


def solution(mesh):
    return jax.shard_map(
        per_device,
        mesh=mesh,
        in_specs=(P(None, "row", "col", None),),
        out_specs=(P(None, "row", None, None, "col", None), P(None, "row", None, None)),
        check_vma=False,
    )
```
